32 devices in a mesh: clips: 2 (over x), tm: 8 (over z, y), head: 2 (over core).
Axes of the slice: x: 2, y: 2, z: 4, core: 2. Of those that a mesh axis runs over, the one named last changes fastest.
Arguments:
- query: bfloat16 [12288, 3072], P(('clips', 'tm'), 'head'), parts along dimension 0, may hold values from -24 to 24
- key: bfloat16 [12288, 3072], P(('clips', 'tm'), 'head'), parts along dimension 0, may hold values from -12 to 12
- value: bfloat16 [12288, 3072], P(('clips', 'tm'), 'head'), parts along dimension 0, may hold values from -6 to 6
- tile_mask: int32 [16, 6, 27], P(('clips', 'tm')), parts along dimension 0, may hold values from 0 to 1, as said below
- order: int32 [16, 768], P(('clips', 'tm')), parts along dimension 0, may hold values from 0 to 767, each once within a row
- out_weight: bfloat16 [3072, 3072], P(None, 'tm'), may hold values from -0.109375 to 0.109375
Outputs:
- mixed: bfloat16 [12288, 3072], P(('clips', 'tm', 'head')), parts along dimension 0
The draws below stay inside these ranges and needn't reach their ends.
There are 2 independent parts, one for each index of `clips`. The reference program is written for one: setup_inputs(seed, part) draws one part's arguments, and reference() takes and returns one part's arrays. A program takes and returns all parts, laid end to end along the dimension named above; an argument that names none is the same for every part. Nothing has to cross between parts.
Inputs may be any that keep to these rules, and one draw needn't show every extreme that they name: `tile_mask`: the tile itself (slot 13) is always 1; slots of neighbours outside the grid of 8 x 2 x 3 tiles are 0. `order`: each row is a permutation of the 768 rows of one time tile's block.
All inputs are finite; a program needn't handle non-finite values.
Results may differ from the reference program's by a relative error of at most 0.0052.
Values may be sent and summed in bfloat16 or wider, within the bound.
A program may use at most 128 MiB of HBM per device.

```python
import jax
import jax.numpy as jnp
from jax import lax

D = 3072
HEADS = 24
HD = 128
GH = 2
GW = 3
TILE_TOK = 128
SLAB = 768
TT = 8
TOKENS = 6144


def draw_key(key, part):
    inner = jax.random.fold_in(key, 21)
    shape = (TOKENS, HEADS, HD)
    spread = jnp.exp(jax.random.uniform(jax.random.fold_in(inner, 1), (TOKENS, 1, 1), jnp.float32, jnp.log(0.3), jnp.log(3.0)))
    result = jax.random.truncated_normal(jax.random.fold_in(inner, 5), -4.0, 4.0, shape, jnp.float32) * spread
    return result.reshape(TOKENS, HEADS * HD).astype(jnp.bfloat16)


def draw_query(key, part):
    inner = jax.random.fold_in(key, 31)
    shape = (TOKENS, HEADS, HD)
    result = jax.random.truncated_normal(jax.random.fold_in(inner, 4), -6.0, 6.0, shape, jnp.float32)
    return result.reshape(TOKENS, HEADS * HD).astype(jnp.bfloat16)


def draw_tile_mask(key, part):
    count = GH * GW
    times = jnp.arange(TT, dtype=jnp.int32)[:, None, None]
    tiles = jnp.arange(count, dtype=jnp.int32)[None, :, None]
    slots = jnp.arange(27, dtype=jnp.int32)[None, None, :]
    shift_time = slots // 9 - 1
    shift_row = slots // 3 % 3 - 1
    shift_col = slots % 3 - 1
    tile_row = tiles // GW
    tile_col = tiles % GW
    inside = (times + shift_time >= 0) & (times + shift_time < TT)
    inside = inside & (tile_row + shift_row >= 0) & (tile_row + shift_row < GH)
    inside = inside & (tile_col + shift_col >= 0) & (tile_col + shift_col < GW)
    keep = jax.random.randint(jax.random.fold_in(key, 41), (TT, count, 27), 0, 4) > 0
    result = jnp.where(slots == 13, 1, jnp.where(inside & keep, 1, 0))
    return result.astype(jnp.int32)


def level_of(stream_key, extent, pieces, low, largest):
    def one(dim, shards_of):
        draws = jax.random.uniform(jax.random.fold_in(jax.random.fold_in(stream_key, 6), dim), (shards_of,), jnp.float32, low / len(pieces), largest / len(pieces))
        return jnp.repeat(jnp.exp(draws), extent[dim] // shards_of).reshape((-1,) + (1,) * (len(extent) - dim - 1))

    factor_of = one(*pieces[0])
    for cut in pieces[1:]:
        factor_of = factor_of * one(*cut)
    return factor_of


def scatter_about(rng, extent, scale, reach, pieces=(), kind=jnp.bfloat16):
    entries = jax.random.normal(rng, extent, jnp.float32) * scale
    if len(pieces) > 0:
        entries = level_of(rng, extent, pieces, -0.22, 0.18) * entries
    return jnp.clip(entries, min=-reach, max=reach).astype(kind)


def setup_inputs(seed: int = 0, part: int = 0) -> dict:
    splits = jax.random.split(jax.random.key(seed), 7)
    part_splits = jax.random.split(jax.random.fold_in(splits[6], part), 7)
    query = draw_query(jax.random.fold_in(jax.random.fold_in(splits[6], part), 71), part)
    key = draw_key(jax.random.fold_in(jax.random.fold_in(splits[6], part), 71), part)
    value = scatter_about(part_splits[2], (TOKENS, HEADS * HD), 1.0, 6.0, ((0, 8), (1, 2)))
    tile_mask = draw_tile_mask(jax.random.fold_in(jax.random.fold_in(splits[6], part), 71), part)
    order = jax.vmap(lambda own: jax.random.permutation(own, SLAB))(jax.random.split(part_splits[4], TT)).reshape((TT, SLAB)).astype(jnp.int32)
    out_weight = scatter_about(splits[5], (HEADS * HD, D), (HEADS * HD) ** -0.5, 0.109375, ((1, 8),))
    return dict(query=query, key=key, value=value, tile_mask=tile_mask, order=order, out_weight=out_weight)


def allowed_tiles(mask_rows, first_tile, total_tiles):
    count = mask_rows.shape[0]
    tiles = jnp.arange(count, dtype=jnp.int32)
    row_diff = tiles[None, :] // GW - tiles[:, None] // GW
    col_diff = tiles[None, :] % GW - tiles[:, None] % GW
    near = (jnp.abs(row_diff) <= 1) & (jnp.abs(col_diff) <= 1)
    slots = jnp.arange(27, dtype=jnp.int32)
    blocks = []
    for shift_time in (-1, 0, 1):
        slot = (shift_time + 1) * 9 + (jnp.clip(row_diff, -1, 1) + 1) * 3 + jnp.clip(col_diff, -1, 1) + 1
        picked = jnp.sum(jnp.where(slot[:, :, None] == slots[None, None, :], mask_rows[:, None, :], 0), axis=2)
        inside = (first_tile + shift_time >= 0) & (first_tile + shift_time < total_tiles)
        blocks.append(near & (picked == 1) & inside)
    return jnp.stack(blocks, axis=1)


def attend(queries, keys, values, allowed, tile_tok):
    rows = queries.shape[0]
    width = queries.shape[1]
    heads = width // HD
    count = allowed.shape[0]
    head_queries = queries.reshape(rows, heads, HD).transpose(1, 0, 2)
    head_keys = keys.reshape(3 * rows, heads, HD).transpose(1, 0, 2)
    head_values = values.reshape(3 * rows, heads, HD).transpose(1, 0, 2)
    visible = allowed.reshape(count, 1, 3 * count, 1)
    scale = HD ** -0.5

    def one_head(inputs):
        part_q, part_k, part_v = inputs
        scores = jnp.dot(part_q, part_k.T, preferred_element_type=jnp.float32) * scale
        scores = scores.reshape(count, tile_tok, 3 * count, tile_tok)
        scores = jnp.where(visible, scores, -jnp.inf)
        top = jnp.max(scores, axis=(2, 3), keepdims=True)
        expon = jnp.exp(scores - top)
        denom = jnp.sum(expon, axis=(2, 3)).reshape(rows, 1)
        weights = expon.reshape(rows, 3 * rows).astype(jnp.bfloat16)
        result = jnp.dot(weights, part_v, preferred_element_type=jnp.float32) / denom
        return result.astype(jnp.bfloat16)

    outputs = lax.map(one_head, (head_queries, head_keys, head_values))
    return outputs.transpose(1, 0, 2).reshape(rows, width)


def reference(query, key, value, tile_mask, order, out_weight):
    slab = GH * GW * TILE_TOK
    width = HEADS * HD

    def to_tiles(data):
        blocks = data.reshape(TT, slab, width)
        return jnp.take_along_axis(blocks, order[:, :, None], axis=1)

    queries = to_tiles(query)
    keys = to_tiles(key)
    values = to_tiles(value)
    empty = jnp.zeros((1, slab, width), key.dtype)
    keys_pad = jnp.concatenate([empty, keys, empty], axis=0)
    values_pad = jnp.concatenate([empty, values, empty], axis=0)

    def one_tile(index):
        window_keys = lax.dynamic_slice_in_dim(keys_pad, index, 3, 0).reshape(3 * slab, width)
        window_values = lax.dynamic_slice_in_dim(values_pad, index, 3, 0).reshape(3 * slab, width)
        allowed = allowed_tiles(tile_mask[index], index, TT)
        return attend(queries[index], window_keys, window_values, allowed, TILE_TOK)

    tiled = lax.map(one_tile, jnp.arange(TT, dtype=jnp.int32))
    restored = jnp.zeros_like(tiled).at[jnp.arange(TT, dtype=jnp.int32)[:, None], order].set(tiled)
    result = jnp.dot(restored.reshape(TT * slab, width), out_weight, preferred_element_type=jnp.float32)
    return result.astype(jnp.bfloat16)
```

```python
import functools
import math

import jax
import jax.numpy as jnp
from jax import lax
from jax.experimental import pallas as pl
from jax.experimental.pallas import tpu as pltpu
from jax.sharding import PartitionSpec as P

HD = 128
GW = 3
CHUNK_HEADS = 2
HIDDEN = -1e30


def allowed_tiles(mask_rows, first_tile, total_tiles):
    count = mask_rows.shape[0]
    tiles = jnp.arange(count, dtype=jnp.int32)
    row_diff = tiles[None, :] // GW - tiles[:, None] // GW
    col_diff = tiles[None, :] % GW - tiles[:, None] % GW
    near = (jnp.abs(row_diff) <= 1) & (jnp.abs(col_diff) <= 1)
    slots = jnp.arange(27, dtype=jnp.int32)
    blocks = []
    for shift_time in (-1, 0, 1):
        slot = (
            (shift_time + 1) * 9
            + (jnp.clip(row_diff, -1, 1) + 1) * 3
            + jnp.clip(col_diff, -1, 1)
            + 1
        )
        picked = jnp.sum(
            jnp.where(slot[:, :, None] == slots[None, None, :], mask_rows[:, None, :], 0), axis=2
        )
        inside = (first_tile + shift_time >= 0) & (first_tile + shift_time < total_tiles)
        blocks.append(near & (picked == 1) & inside)
    return blocks


def reorder_kernel(pick_ref, a_ref, o_ref):
    o_ref[...] = jnp.dot(
        pick_ref[...], a_ref[...], preferred_element_type=jnp.float32
    ).astype(o_ref.dtype)


def reorder_pair_kernel(pick_ref, k_ref, v_ref, o_ref):
    width = k_ref.shape[1]
    pick = pick_ref[...]
    for index, ref in enumerate((k_ref, v_ref)):
        o_ref[:, index * width : (index + 1) * width] = jnp.dot(
            pick, ref[...], preferred_element_type=jnp.float32
        ).astype(o_ref.dtype)


def reorder(pick, data):
    rows, width = data.shape
    step = 512 if width % 512 == 0 else HD
    return pl.pallas_call(
        reorder_kernel,
        grid=(width // step,),
        in_specs=[
            pl.BlockSpec((rows, rows), lambda i: (0, 0)),
            pl.BlockSpec((rows, step), lambda i: (0, i)),
        ],
        out_specs=pl.BlockSpec((rows, step), lambda i: (0, i)),
        out_shape=jax.ShapeDtypeStruct((rows, width), data.dtype),
        cost_estimate=pl.CostEstimate(
            flops=2 * rows * rows * width, bytes_accessed=4 * rows * width, transcendentals=0
        ),
        name="reorder",
    )(pick, data)


def reorder_pair(pick, key, value, chunk, step):
    rows = key.shape[0]
    return pl.pallas_call(
        reorder_pair_kernel,
        grid=(1,),
        in_specs=[
            pl.BlockSpec((rows, rows), lambda i: (0, 0)),
            pl.BlockSpec((rows, step), lambda i: (0, chunk)),
            pl.BlockSpec((rows, step), lambda i: (0, chunk)),
        ],
        out_specs=pl.BlockSpec((rows, 2 * step), lambda i: (0, 0)),
        out_shape=jax.ShapeDtypeStruct((rows, 2 * step), key.dtype),
        cost_estimate=pl.CostEstimate(
            flops=4 * rows * rows * step, bytes_accessed=8 * rows * step, transcendentals=0
        ),
        name="reorder_pair",
    )(pick, key, value)


def attend_kernel(tile_tok, q_ref, *refs):
    k_refs, v_refs = refs[0:3], refs[3:6]
    bias_ref, back_ref, own_ref, other_ref, att_ref = refs[6:]
    rows = q_ref.shape[0]
    half = rows // 2
    factor = HD ** (-0.5) * math.log2(math.e)
    dims = (((1,), (1,)), ((), ()))
    for tile in range(rows // tile_tok):
        part_q = q_ref[tile * tile_tok : (tile + 1) * tile_tok, :]
        scores = [
            lax.dot_general(part_q, k_ref[...], dims, preferred_element_type=jnp.float32) * factor
            + bias_ref[tile : tile + 1, index * rows : (index + 1) * rows]
            for index, k_ref in enumerate(k_refs)
        ]
        top = functools.reduce(
            jnp.maximum, [jnp.max(part, axis=1, keepdims=True) for part in scores]
        )
        total = 0.0
        denom = 0.0
        for part, v_ref in zip(scores, v_refs):
            expon = jnp.exp2(part - top)
            denom = denom + jnp.sum(expon, axis=1, keepdims=True)
            total = total + jnp.dot(
                expon.astype(jnp.bfloat16), v_ref[...], preferred_element_type=jnp.float32
            )
        att_ref[tile * tile_tok : (tile + 1) * tile_tok, :] = (total / denom).astype(jnp.bfloat16)
    att = att_ref[...]
    own_ref[...] = jnp.dot(
        back_ref[:half, :], att, preferred_element_type=jnp.float32
    ).astype(jnp.bfloat16)
    other_ref[...] = jnp.dot(
        back_ref[half:, :], att, preferred_element_type=jnp.float32
    ).astype(jnp.bfloat16)


def attend(queries, pairs, bias, back, chunk, tile_tok):
    rows = queries.shape[0]
    heads = pairs[0].shape[1] // (2 * HD)
    column = lambda i: (0, i)
    later = lambda i: (0, heads + i)
    whole = lambda i: (0, 0)
    in_specs = [pl.BlockSpec((rows, HD), lambda i: (0, chunk * heads + i))]
    in_specs += [pl.BlockSpec((rows, HD), column)] * 3
    in_specs += [pl.BlockSpec((rows, HD), later)] * 3
    in_specs += [pl.BlockSpec(bias.shape, whole), pl.BlockSpec(back.shape, whole)]
    half = jax.ShapeDtypeStruct((rows // 2, heads * HD), queries.dtype)
    return pl.pallas_call(
        functools.partial(attend_kernel, tile_tok),
        grid=(heads,),
        in_specs=in_specs,
        out_specs=[pl.BlockSpec((rows // 2, HD), column)] * 2,
        out_shape=[half, half],
        scratch_shapes=[pltpu.VMEM((rows, HD), jnp.bfloat16)],
        compiler_params=pltpu.CompilerParams(vmem_limit_bytes=48 << 20),
        cost_estimate=pl.CostEstimate(
            flops=4 * heads * rows * 3 * rows * HD * 2,
            bytes_accessed=16 * rows * heads * HD,
            transcendentals=heads * rows * 3 * rows,
        ),
        name="attend",
    )(queries, *pairs, *pairs, bias, back)


def project_kernel(count, *refs):
    pieces, (own_ref, other_ref, out_ref, all_ref) = refs[: 2 * count], refs[2 * count :]
    step = pieces[0].shape[1]
    depth = own_ref.shape[1]

    @pl.when(pl.program_id(0) == 0)
    def _():
        for index, piece in enumerate(pieces):
            all_ref[:, index * step : (index + 1) * step] = piece[...]

    width = own_ref.shape[2]
    for block in range(own_ref.shape[0]):
        total = jnp.dot(all_ref[:, :depth], own_ref[block], preferred_element_type=jnp.float32)
        total += jnp.dot(all_ref[:, depth:], other_ref[block], preferred_element_type=jnp.float32)
        out_ref[:, block * width : (block + 1) * width] = total.astype(out_ref.dtype)


def project(own, other, weight_own, weight_other):
    count = len(own)
    rows, step = own[0].shape
    blocks, depth, width = weight_own.shape
    group = 1 if width % 128 == 0 else 2
    whole = lambda i: (0, 0)
    each = lambda i: (i, 0, 0)
    return pl.pallas_call(
        functools.partial(project_kernel, count),
        grid=(blocks // group,),
        in_specs=[pl.BlockSpec((rows, step), whole)] * (2 * count)
        + [pl.BlockSpec((group, depth, width), each)] * 2,
        out_specs=pl.BlockSpec((rows, group * width), lambda i: (0, i)),
        out_shape=jax.ShapeDtypeStruct((rows, blocks * width), jnp.bfloat16),
        scratch_shapes=[pltpu.VMEM((rows, 2 * depth), jnp.bfloat16)],
        compiler_params=pltpu.CompilerParams(vmem_limit_bytes=48 << 20),
        cost_estimate=pl.CostEstimate(
            flops=4 * rows * depth * blocks * width,
            bytes_accessed=4 * depth * blocks * width,
            transcendentals=0,
        ),
        name="project",
    )(*own, *other, weight_own, weight_other)


def on_device(query, key, value, tile_mask, order, out_weight):
    slab = order.shape[1]
    tile_tok = slab // tile_mask.shape[1]
    width = query.shape[1]
    step = CHUNK_HEADS * HD
    count = lax.axis_size("tm")
    me = lax.axis_index("tm")
    side = lax.axis_index("head")
    even = me % 2 == 0

    beside = [(i, i ^ 1) for i in range(count)]
    onward = [(i, i + 2) for i in range(0, count - 2, 2)]
    onward += [(i, i - 2) for i in range(3, count, 2)]
    across = [(0, 1), (1, 0)]

    depth = out_weight.shape[0] // 2
    rows_own = lax.dynamic_slice_in_dim(out_weight, side * depth, depth, 0)
    weight_own = lax.all_gather(rows_own, "tm", axis=0, tiled=False)
    weight_other = lax.ppermute(weight_own, "head", across)

    places = jnp.arange(slab, dtype=jnp.int32)
    pick = (order[0][:, None] == places[None, :]).astype(jnp.bfloat16)
    half = slab // 2
    targets = (places + side * half) % slab
    back = (targets[:, None] == order[0][None, :]).astype(jnp.bfloat16)

    low, mid, high = allowed_tiles(tile_mask[0], me, count)
    seen = jnp.concatenate([mid, jnp.where(even, high, low), jnp.where(even, low, high)], axis=1)
    bias = jnp.repeat(jnp.where(seen, 0.0, HIDDEN).astype(jnp.float32), tile_tok, axis=1)

    chunks = range(width // step)
    mine = [reorder_pair(pick, key, value, chunk, step) for chunk in chunks]
    near = [lax.ppermute(pair, "tm", beside) for pair in mine]
    far = [lax.ppermute(pair, "tm", onward) for pair in near]
    queries = reorder(pick, query)

    own, other = [], []
    for chunk in chunks:
        kept, sent = attend(
            queries, (mine[chunk], near[chunk], far[chunk]), bias, back, chunk, tile_tok
        )
        own.append(kept)
        other.append(lax.ppermute(sent, "head", across))
    return project(own, other, weight_own, weight_other)


def solution(mesh):
    placed = (
        P(("clips", "tm"), "head"),
        P(("clips", "tm"), "head"),
        P(("clips", "tm"), "head"),
        P(("clips", "tm"), None, None),
        P(("clips", "tm"), None),
        P(None, "tm"),
    )
    return jax.shard_map(
        on_device,
        mesh=mesh,
        in_specs=placed,
        out_specs=P(("clips", "tm", "head"), None),
        check_vma=False,
    )
```

```python
import functools
import math

import jax
import jax.numpy as jnp
from jax import lax
from jax.experimental import pallas as pl
from jax.experimental.pallas import tpu as pltpu
from jax.sharding import PartitionSpec as P

HD = 128
GW = 3
PIECES = 2
TIES = (1, 3)
HIDDEN = -1e30


def allowed_tiles(mask_rows, first_tile, total_tiles):
    count = mask_rows.shape[0]
    tiles = jnp.arange(count, dtype=jnp.int32)
    row_diff = tiles[None, :] // GW - tiles[:, None] // GW
    col_diff = tiles[None, :] % GW - tiles[:, None] % GW
    near = (jnp.abs(row_diff) <= 1) & (jnp.abs(col_diff) <= 1)
    slots = jnp.arange(27, dtype=jnp.int32)
    blocks = []
    for shift_time in (-1, 0, 1):
        slot = (
            (shift_time + 1) * 9
            + (jnp.clip(row_diff, -1, 1) + 1) * 3
            + jnp.clip(col_diff, -1, 1)
            + 1
        )
        picked = jnp.sum(
            jnp.where(slot[:, :, None] == slots[None, None, :], mask_rows[:, None, :], 0), axis=2
        )
        inside = (first_tile + shift_time >= 0) & (first_tile + shift_time < total_tiles)
        blocks.append(near & (picked == 1) & inside)
    return blocks


def reorder_kernel(pick_ref, a_ref, o_ref):
    o_ref[...] = jnp.dot(
        pick_ref[...], a_ref[...], preferred_element_type=jnp.float32
    ).astype(o_ref.dtype)


def reorder_pair_kernel(pick_ref, k_ref, v_ref, o_ref):
    width = k_ref.shape[1]
    pick = pick_ref[...]
    for index, ref in enumerate((k_ref, v_ref)):
        o_ref[:, index * width : (index + 1) * width] = jnp.dot(
            pick, ref[...], preferred_element_type=jnp.float32
        ).astype(o_ref.dtype)


def reorder(pick, data):
    rows, width = data.shape
    step = 512 if width % 512 == 0 else HD
    return pl.pallas_call(
        reorder_kernel,
        grid=(width // step,),
        in_specs=[
            pl.BlockSpec((rows, rows), lambda i: (0, 0)),
            pl.BlockSpec((rows, step), lambda i: (0, i)),
        ],
        out_specs=pl.BlockSpec((rows, step), lambda i: (0, i)),
        out_shape=jax.ShapeDtypeStruct((rows, width), data.dtype),
        cost_estimate=pl.CostEstimate(
            flops=2 * rows * rows * width, bytes_accessed=4 * rows * width, transcendentals=0
        ),
        name="reorder",
    )(pick, data)


def reorder_pair(pick, key, value, chunk, step):
    rows = key.shape[0]
    return pl.pallas_call(
        reorder_pair_kernel,
        grid=(1,),
        in_specs=[
            pl.BlockSpec((rows, rows), lambda i: (0, 0)),
            pl.BlockSpec((rows, step), lambda i: (0, chunk)),
            pl.BlockSpec((rows, step), lambda i: (0, chunk)),
        ],
        out_specs=pl.BlockSpec((rows, 2 * step), lambda i: (0, 0)),
        out_shape=jax.ShapeDtypeStruct((rows, 2 * step), key.dtype),
        cost_estimate=pl.CostEstimate(
            flops=4 * rows * rows * step, bytes_accessed=8 * rows * step, transcendentals=0
        ),
        name="reorder_pair",
    )(pick, key, value)


def attend_kernel(tile_tok, q_ref, *refs):
    k_refs, v_refs = refs[0:3], refs[3:6]
    bias_ref, back_ref, own_ref, other_ref, att_ref = refs[6:]
    rows = q_ref.shape[0]
    half = rows // 2
    factor = HD ** (-0.5) * math.log2(math.e)
    dims = (((1,), (1,)), ((), ()))

    @pl.loop(0, rows // tile_tok)
    def _(tile):
        place = pl.ds(pl.multiple_of(tile * tile_tok, tile_tok), tile_tok)
        part_q = q_ref[place, :]
        scores = [
            lax.dot_general(part_q, k_ref[...], dims, preferred_element_type=jnp.float32) * factor
            + bias_ref[pl.ds(tile, 1), index * rows : (index + 1) * rows]
            for index, k_ref in enumerate(k_refs)
        ]
        top = functools.reduce(
            jnp.maximum, [jnp.max(part, axis=1, keepdims=True) for part in scores]
        )
        total = 0.0
        denom = 0.0
        for part, v_ref in zip(scores, v_refs):
            expon = jnp.exp2(part - top)
            denom = denom + jnp.sum(expon, axis=1, keepdims=True)
            total = total + jnp.dot(
                expon.astype(jnp.bfloat16), v_ref[...], preferred_element_type=jnp.float32
            )
        att_ref[place, :] = (total / denom).astype(jnp.bfloat16)

    att = att_ref[...]
    own_ref[...] = jnp.dot(
        back_ref[:half, :], att, preferred_element_type=jnp.float32
    ).astype(jnp.bfloat16)
    other_ref[...] = jnp.dot(
        back_ref[half:, :], att, preferred_element_type=jnp.float32
    ).astype(jnp.bfloat16)


def attend(queries, pairs, bias, back, chunk, tile_tok):
    rows = queries.shape[0]
    heads = pairs[0].shape[1] // (2 * HD)
    column = lambda i: (0, i)
    later = lambda i: (0, heads + i)
    whole = lambda i: (0, 0)
    in_specs = [pl.BlockSpec((rows, HD), lambda i: (0, chunk * heads + i))]
    in_specs += [pl.BlockSpec((rows, HD), column)] * 3
    in_specs += [pl.BlockSpec((rows, HD), later)] * 3
    in_specs += [pl.BlockSpec(bias.shape, whole), pl.BlockSpec(back.shape, whole)]
    half = jax.ShapeDtypeStruct((rows // 2, heads * HD), queries.dtype)
    return pl.pallas_call(
        functools.partial(attend_kernel, tile_tok),
        grid=(heads,),
        in_specs=in_specs,
        out_specs=[pl.BlockSpec((rows // 2, HD), column)] * 2,
        out_shape=[half, half],
        scratch_shapes=[pltpu.VMEM((rows, HD), jnp.bfloat16)],
        compiler_params=pltpu.CompilerParams(vmem_limit_bytes=48 << 20),
        cost_estimate=pl.CostEstimate(
            flops=4 * heads * rows * 3 * rows * HD * 2,
            bytes_accessed=16 * rows * heads * HD,
            transcendentals=heads * rows * 3 * rows,
        ),
        name="attend",
    )(queries, *pairs, *pairs, bias, back)


def project_kernel(count, starts, shift_ref, *refs):
    pieces, weights = refs[: 2 * count], refs[2 * count : -2]
    out_ref, all_ref = refs[-2:]
    depth = all_ref.shape[1] // 2
    part = weights[0].shape[1]
    width = weights[0].shape[2]

    @pl.when(pl.program_id(0) == 0)
    def _():
        for index, piece in enumerate(pieces):
            side, place = index // count, starts[index % count]
            column = side * depth + lax.rem(place + shift_ref[0], depth)
            all_ref[:, pl.ds(pl.multiple_of(column, HD), piece.shape[1])] = piece[...]

    for block in range(weights[0].shape[0]):
        total = 0.0
        for index, weight in enumerate(weights):
            total = total + jnp.dot(
                all_ref[:, index * part : (index + 1) * part],
                weight[block],
                preferred_element_type=jnp.float32,
            )
        out_ref[:, block * width : (block + 1) * width] = total.astype(out_ref.dtype)


def project(own, other, starts, shift, weights):
    count = len(own)
    rows = own[0].shape[0]
    blocks, part, width = weights[0].shape
    depth = part * len(weights)
    group = 1 if width % 128 == 0 else 2
    return pl.pallas_call(
        functools.partial(project_kernel, count, starts),
        grid=(blocks // group,),
        in_specs=[pl.BlockSpec(memory_space=pltpu.SMEM)]
        + [pl.BlockSpec(piece.shape, lambda i: (0, 0)) for piece in own + other]
        + [pl.BlockSpec((group, part, width), lambda i: (i, 0, 0))] * len(weights),
        out_specs=pl.BlockSpec((rows, group * width), lambda i: (0, i)),
        out_shape=jax.ShapeDtypeStruct((rows, blocks * width), jnp.bfloat16),
        scratch_shapes=[pltpu.VMEM((rows, depth), jnp.bfloat16)],
        compiler_params=pltpu.CompilerParams(vmem_limit_bytes=48 << 20),
        cost_estimate=pl.CostEstimate(
            flops=2 * rows * depth * blocks * width,
            bytes_accessed=2 * depth * blocks * width,
            transcendentals=0,
        ),
        name="project",
    )(shift, *own, *other, *weights)


def on_device(query, key, value, tile_mask, order, out_weight):
    slab = order.shape[1]
    tile_tok = slab // tile_mask.shape[1]
    width = query.shape[1]
    count = lax.axis_size("tm")
    me = lax.axis_index("tm")
    side = lax.axis_index("head")
    even = me % 2 == 0

    beside = [(i, i ^ 1) for i in range(count)]
    onward = [(i, i + 2) for i in range(0, count - 2, 2)]
    onward += [(i, i - 2) for i in range(3, count, 2)]
    across = [(0, 1), (1, 0)]

    clip = lax.axis_index("clips") % 2
    paired = [(i, i ^ 1) for i in range(lax.axis_size("clips"))]
    depth = out_weight.shape[0] // 2
    part = depth // (2 * PIECES)
    gathered = []
    for piece in range(PIECES):
        start = side * depth + clip * (depth // 2) + piece * part
        rows = lax.dynamic_slice_in_dim(out_weight, start, part, 0)
        gathered.append(lax.all_gather(rows, "tm", axis=0, tiled=False))

    places = jnp.arange(slab, dtype=jnp.int32)
    pick = (order[0][:, None] == places[None, :]).astype(jnp.bfloat16)
    half = slab // 2
    targets = (places + side * half) % slab
    back = (targets[:, None] == order[0][None, :]).astype(jnp.bfloat16)

    low, mid, high = allowed_tiles(tile_mask[0], me, count)
    seen = jnp.concatenate([mid, jnp.where(even, high, low), jnp.where(even, low, high)], axis=1)
    bias = jnp.repeat(jnp.where(seen, 0.0, HIDDEN).astype(jnp.float32), tile_tok, axis=1)

    heads = width // HD
    sizes = [2] * (heads // 2 - 1) + [1, 1]
    starts = [sum(sizes[:index]) for index in range(len(sizes))]
    chunks = range(len(sizes))
    mine = []
    for start, size in zip(starts, sizes):
        pair = reorder_pair(pick, key, value, start // size, size * HD)
        pick, pair = lax.optimization_barrier((pick, pair))
        mine.append(pair)
    near = [lax.ppermute(pair, "tm", beside) for pair in mine]
    far = [lax.ppermute(pair, "tm", onward) for pair in near]
    queries = reorder(pick, query)

    own, other, crossed = [], [], []
    for chunk in chunks:
        ahead = min(chunk + 2, len(sizes) - 1)
        queries, near[ahead] = lax.optimization_barrier((queries, near[ahead]))
        if chunk == TIES[1] + 2:
            queries, crossed[0] = lax.optimization_barrier((queries, crossed[0]))
        kept, sent = attend(
            queries,
            (mine[chunk], near[chunk], far[chunk]),
            bias,
            back,
            starts[chunk] // sizes[chunk],
            tile_tok,
        )
        queries, kept = lax.optimization_barrier((queries, kept))
        if chunk in TIES:
            piece = TIES.index(chunk)
            gathered[piece], kept = lax.optimization_barrier((gathered[piece], kept))
            crossed.append(lax.ppermute(gathered[piece], "clips", paired))
        own.append(kept)
        other.append(lax.ppermute(sent, "head", across))
    weights = gathered + crossed
    weights = weights + [lax.ppermute(weight, "head", across) for weight in weights]
    shift = (clip * (depth // 2)).astype(jnp.int32).reshape(1)
    return project(own, other, [start * HD for start in starts], shift, weights)


def solution(mesh):
    placed = (
        P(("clips", "tm"), "head"),
        P(("clips", "tm"), "head"),
        P(("clips", "tm"), "head"),
        P(("clips", "tm"), None, None),
        P(("clips", "tm"), None),
        P(None, "tm"),
    )
    return jax.shard_map(
        on_device,
        mesh=mesh,
        in_specs=placed,
        out_specs=P(("clips", "tm", "head"), None),
        check_vma=False,
    )
```

```python
import functools
import math

import jax
import jax.numpy as jnp
from jax import lax
from jax.experimental import pallas as pl
from jax.experimental.pallas import tpu as pltpu
from jax.sharding import PartitionSpec as P

HD = 128
GW = 3
PIECES = 2
TIES = (0, 2)
HIDDEN = -1e30


def allowed_tiles(mask_rows, first_tile, total_tiles):
    count = mask_rows.shape[0]
    tiles = jnp.arange(count, dtype=jnp.int32)
    row_diff = tiles[None, :] // GW - tiles[:, None] // GW
    col_diff = tiles[None, :] % GW - tiles[:, None] % GW
    near = (jnp.abs(row_diff) <= 1) & (jnp.abs(col_diff) <= 1)
    slots = jnp.arange(27, dtype=jnp.int32)
    blocks = []
    for shift_time in (-1, 0, 1):
        slot = (
            (shift_time + 1) * 9
            + (jnp.clip(row_diff, -1, 1) + 1) * 3
            + jnp.clip(col_diff, -1, 1)
            + 1
        )
        picked = jnp.sum(
            jnp.where(slot[:, :, None] == slots[None, None, :], mask_rows[:, None, :], 0), axis=2
        )
        inside = (first_tile + shift_time >= 0) & (first_tile + shift_time < total_tiles)
        blocks.append(near & (picked == 1) & inside)
    return blocks


def reorder_kernel(pick_ref, a_ref, o_ref):
    o_ref[...] = jnp.dot(
        pick_ref[...], a_ref[...], preferred_element_type=jnp.float32
    ).astype(o_ref.dtype)


def reorder_pair_kernel(pick_ref, k_ref, v_ref, o_ref):
    width = k_ref.shape[1]
    pick = pick_ref[...]
    for index, ref in enumerate((k_ref, v_ref)):
        o_ref[:, index * width : (index + 1) * width] = jnp.dot(
            pick, ref[...], preferred_element_type=jnp.float32
        ).astype(o_ref.dtype)


def reorder(pick, data):
    rows, width = data.shape
    step = 512 if width % 512 == 0 else HD
    return pl.pallas_call(
        reorder_kernel,
        grid=(width // step,),
        in_specs=[
            pl.BlockSpec((rows, rows), lambda i: (0, 0)),
            pl.BlockSpec((rows, step), lambda i: (0, i)),
        ],
        out_specs=pl.BlockSpec((rows, step), lambda i: (0, i)),
        out_shape=jax.ShapeDtypeStruct((rows, width), data.dtype),
        cost_estimate=pl.CostEstimate(
            flops=2 * rows * rows * width, bytes_accessed=4 * rows * width, transcendentals=0
        ),
        name="reorder",
    )(pick, data)


def reorder_pair(pick, key, value, chunk, step):
    rows = key.shape[0]
    return pl.pallas_call(
        reorder_pair_kernel,
        grid=(1,),
        in_specs=[
            pl.BlockSpec((rows, rows), lambda i: (0, 0)),
            pl.BlockSpec((rows, step), lambda i: (0, chunk)),
            pl.BlockSpec((rows, step), lambda i: (0, chunk)),
        ],
        out_specs=pl.BlockSpec((rows, 2 * step), lambda i: (0, 0)),
        out_shape=jax.ShapeDtypeStruct((rows, 2 * step), key.dtype),
        cost_estimate=pl.CostEstimate(
            flops=4 * rows * rows * step, bytes_accessed=8 * rows * step, transcendentals=0
        ),
        name="reorder_pair",
    )(pick, key, value)


def attend_kernel(tile_tok, q_ref, *refs):
    k_refs, v_refs = refs[0:3], refs[3:6]
    bias_ref, back_ref, own_ref, other_ref, att_ref = refs[6:]
    rows = q_ref.shape[0]
    half = rows // 2
    factor = HD ** (-0.5) * math.log2(math.e)
    dims = (((1,), (1,)), ((), ()))

    def one_tile(tile):
        place = pl.ds(pl.multiple_of(tile * tile_tok, tile_tok), tile_tok)
        part_q = q_ref[place, :]
        scores = [
            lax.dot_general(part_q, k_ref[...], dims, preferred_element_type=jnp.float32) * factor
            + bias_ref[pl.ds(tile, 1), index * rows : (index + 1) * rows]
            for index, k_ref in enumerate(k_refs)
        ]
        top = functools.reduce(
            jnp.maximum, [jnp.max(part, axis=1, keepdims=True) for part in scores]
        )
        total = 0.0
        denom = 0.0
        for part, v_ref in zip(scores, v_refs):
            expon = jnp.exp2(part - top)
            denom = denom + jnp.sum(expon, axis=1, keepdims=True)
            total = total + jnp.dot(
                expon.astype(jnp.bfloat16), v_ref[...], preferred_element_type=jnp.float32
            )
        att_ref[place, :] = (total / denom).astype(jnp.bfloat16)

    @pl.loop(0, rows // (2 * tile_tok))
    def _(index):
        one_tile(2 * index)
        one_tile(2 * index + 1)

    att = att_ref[...]
    own_ref[...] = jnp.dot(
        back_ref[:half, :], att, preferred_element_type=jnp.float32
    ).astype(jnp.bfloat16)
    other_ref[...] = jnp.dot(
        back_ref[half:, :], att, preferred_element_type=jnp.float32
    ).astype(jnp.bfloat16)


def attend(queries, pairs, bias, back, chunk, tile_tok):
    rows = queries.shape[0]
    heads = pairs[0].shape[1] // (2 * HD)
    column = lambda i: (0, i)
    later = lambda i: (0, heads + i)
    whole = lambda i: (0, 0)
    in_specs = [pl.BlockSpec((rows, HD), lambda i: (0, chunk * heads + i))]
    in_specs += [pl.BlockSpec((rows, HD), column)] * 3
    in_specs += [pl.BlockSpec((rows, HD), later)] * 3
    in_specs += [pl.BlockSpec(bias.shape, whole), pl.BlockSpec(back.shape, whole)]
    half = jax.ShapeDtypeStruct((rows // 2, heads * HD), queries.dtype)
    return pl.pallas_call(
        functools.partial(attend_kernel, tile_tok),
        grid=(heads,),
        in_specs=in_specs,
        out_specs=[pl.BlockSpec((rows // 2, HD), column)] * 2,
        out_shape=[half, half],
        scratch_shapes=[pltpu.VMEM((rows, HD), jnp.bfloat16)],
        compiler_params=pltpu.CompilerParams(vmem_limit_bytes=48 << 20),
        cost_estimate=pl.CostEstimate(
            flops=4 * heads * rows * 3 * rows * HD * 2,
            bytes_accessed=16 * rows * heads * HD,
            transcendentals=heads * rows * 3 * rows,
        ),
        name="attend",
    )(queries, *pairs, *pairs, bias, back)


def project_kernel(count, starts, shift_ref, *refs):
    pieces, weights = refs[: 2 * count], refs[2 * count : -2]
    out_ref, all_ref = refs[-2:]
    depth = all_ref.shape[1] // 2
    part = weights[0].shape[1]
    width = weights[0].shape[2]

    @pl.when(pl.program_id(0) == 0)
    def _():
        for index, piece in enumerate(pieces):
            side, place = index // count, starts[index % count]
            column = side * depth + lax.rem(place + shift_ref[0], depth)
            all_ref[:, pl.ds(pl.multiple_of(column, HD), piece.shape[1])] = piece[...]

    for block in range(weights[0].shape[0]):
        total = 0.0
        for index, weight in enumerate(weights):
            total = total + jnp.dot(
                all_ref[:, index * part : (index + 1) * part],
                weight[block],
                preferred_element_type=jnp.float32,
            )
        out_ref[:, block * width : (block + 1) * width] = total.astype(out_ref.dtype)


def project(own, other, starts, shift, weights):
    count = len(own)
    rows = own[0].shape[0]
    blocks, part, width = weights[0].shape
    depth = part * len(weights)
    group = 1 if width % 128 == 0 else 2
    return pl.pallas_call(
        functools.partial(project_kernel, count, starts),
        grid=(blocks // group,),
        in_specs=[pl.BlockSpec(memory_space=pltpu.SMEM)]
        + [pl.BlockSpec(piece.shape, lambda i: (0, 0)) for piece in own + other]
        + [pl.BlockSpec((group, part, width), lambda i: (i, 0, 0))] * len(weights),
        out_specs=pl.BlockSpec((rows, group * width), lambda i: (0, i)),
        out_shape=jax.ShapeDtypeStruct((rows, blocks * width), jnp.bfloat16),
        scratch_shapes=[pltpu.VMEM((rows, depth), jnp.bfloat16)],
        compiler_params=pltpu.CompilerParams(vmem_limit_bytes=48 << 20),
        cost_estimate=pl.CostEstimate(
            flops=2 * rows * depth * blocks * width,
            bytes_accessed=2 * depth * blocks * width,
            transcendentals=0,
        ),
        name="project",
    )(shift, *own, *other, *weights)


def on_device(query, key, value, tile_mask, order, out_weight):
    slab = order.shape[1]
    tile_tok = slab // tile_mask.shape[1]
    width = query.shape[1]
    count = lax.axis_size("tm")
    me = lax.axis_index("tm")
    side = lax.axis_index("head")
    even = me % 2 == 0

    beside = [(i, i ^ 1) for i in range(count)]
    onward = [(i, i + 2) for i in range(0, count - 2, 2)]
    onward += [(i, i - 2) for i in range(3, count, 2)]
    across = [(0, 1), (1, 0)]

    clip = lax.axis_index("clips") % 2
    paired = [(i, i ^ 1) for i in range(lax.axis_size("clips"))]
    depth = out_weight.shape[0] // 2
    part = depth // (2 * PIECES)
    gathered = []
    for piece in range(PIECES):
        start = side * depth + clip * (depth // 2) + piece * part
        rows = lax.dynamic_slice_in_dim(out_weight, start, part, 0)
        gathered.append(lax.all_gather(rows, "tm", axis=0, tiled=False))

    places = jnp.arange(slab, dtype=jnp.int32)
    pick = (order[0][:, None] == places[None, :]).astype(jnp.bfloat16)
    half = slab // 2
    targets = (places + side * half) % slab
    back = (targets[:, None] == order[0][None, :]).astype(jnp.bfloat16)

    low, mid, high = allowed_tiles(tile_mask[0], me, count)
    seen = jnp.concatenate([mid, jnp.where(even, high, low), jnp.where(even, low, high)], axis=1)
    bias = jnp.repeat(jnp.where(seen, 0.0, HIDDEN).astype(jnp.float32), tile_tok, axis=1)

    heads = width // HD
    sizes = [2] * (heads // 2 - 1) + [1, 1]
    starts = [sum(sizes[:index]) for index in range(len(sizes))]
    chunks = range(len(sizes))
    mine = []
    for start, size in zip(starts, sizes):
        pair = reorder_pair(pick, key, value, start // size, size * HD)
        pick, pair = lax.optimization_barrier((pick, pair))
        mine.append(pair)
    near = [lax.ppermute(pair, "tm", beside) for pair in mine]
    far = [lax.ppermute(pair, "tm", onward) for pair in near]
    queries = reorder(pick, query)

    own, other, crossed = [], [], []
    for chunk in chunks:
        ahead = min(chunk + 2, len(sizes) - 1)
        queries, near[ahead] = lax.optimization_barrier((queries, near[ahead]))
        after = min(chunk + 1, len(sizes) - 1)
        queries, far[after] = lax.optimization_barrier((queries, far[after]))
        if chunk in TIES:
            piece = TIES.index(chunk)
            queries, gathered[piece] = lax.optimization_barrier((queries, gathered[piece]))
            crossed.append(lax.ppermute(gathered[piece], "clips", paired))
        if chunk == len(sizes) - 2:
            queries, crossed[0] = lax.optimization_barrier((queries, crossed[0]))
        kept, sent = attend(
            queries,
            (mine[chunk], near[chunk], far[chunk]),
            bias,
            back,
            starts[chunk] // sizes[chunk],
            tile_tok,
        )
        queries, kept = lax.optimization_barrier((queries, kept))
        own.append(kept)
        other.append(lax.ppermute(sent, "head", across))
    weights = gathered + crossed
    weights = weights + [lax.ppermute(weight, "head", across) for weight in weights]
    shift = (clip * (depth // 2)).astype(jnp.int32).reshape(1)
    return project(own, other, [start * HD for start in starts], shift, weights)


def solution(mesh):
    placed = (
        P(("clips", "tm"), "head"),
        P(("clips", "tm"), "head"),
        P(("clips", "tm"), "head"),
        P(("clips", "tm"), None, None),
        P(("clips", "tm"), None),
        P(None, "tm"),
    )
    return jax.shard_map(
        on_device,
        mesh=mesh,
        in_specs=placed,
        out_specs=P(("clips", "tm", "head"), None),
        check_vma=False,
    )
```
